32 devices in a mesh: expert: 8 (over z, y), dp: 4 (over x, core).
Axes of the slice: x: 2, y: 2, z: 4, core: 2. Of those that a mesh axis runs over, the one named last changes fastest.
Arguments:
- tokens: bfloat16 [512, 7168], P('expert'), may hold values from -6 to 6
- expert_ids: int32 [512, 8], P('expert'), may hold values from 0 to 31, all different within a row; in each aligned block of 64 rows (0 to 63, 64 to 127, ...) at most 24 rows name the same one
- gate_weights: bfloat16 [512, 8], P('expert'), may hold values from 0.19921875 to 1
- w_gate: bfloat16 [32, 7168, 2048], P('expert', None, 'dp'), may hold values from -0.0625 to 0.0625
- w_up: bfloat16 [32, 7168, 2048], P('expert', None, 'dp'), may hold values from -0.0625 to 0.0625
- w_down: bfloat16 [32, 2048, 7168], P('expert', 'dp'), may hold values from -0.125 to 0.125
Outputs:
- layer_output: bfloat16 [512, 7168], P('expert')
The draws below stay inside these ranges and needn't reach their ends.
Inputs may be any that keep to these rules, and one draw needn't show every extreme that they name: `expert_ids`: each token names 8 different experts. Among the 64 tokens of one index of expert (aligned blocks of rows), no expert is named more than 24 times, and in some blocks an expert is named exactly 24 times.
All inputs are finite; a program needn't handle non-finite values.
Results may differ from the reference program's by a relative error of at most 0.013.
Values may be sent and summed in bfloat16 or wider, within the bound.
No kernel may reach another device: no remote copies, remote signals or barrier semaphores. Data moves between devices by JAX's collectives and lax.ppermute only.
A program may use at most 192 MiB of HBM per device.

```python
import math
import jax
import jax.numpy as jnp
import numpy as np
from jax import lax

D = 7168
FF = 2048
EXPERTS = 32
TOP = 8
TOK_DEV = 64
CAP = 24
TOKENS = 512
N_DP = 4


def steps_of(rng, extent, shards, smallest, largest):
    level = 1.0
    for axis_at, shards_of in shards:
        draws = jax.random.uniform(jax.random.fold_in(jax.random.fold_in(rng, 6), axis_at), (shards_of,), jnp.float32, smallest / len(shards), largest / len(shards))
        level = level * jnp.repeat(jnp.exp(draws), extent[axis_at] // shards_of).reshape((-1,) + (1,) * (len(extent) - 1 - axis_at))
    return level


def routed_block(rng, own, number, rows, count, top, reach, slope):
    sequence = jax.random.permutation(rng, count)
    heavy_load, common = portions_of(count, rows * top, reach, slope, True), portions_of(count, rows * top, reach, slope, False)
    places = jnp.arange(count)

    def named(tallies, offset_by):
        used = int((tallies > 0).sum())
        fixed = max(1, used // 4)
        passed = fixed + (places - fixed + offset_by * (used - fixed)) % max(1, count - fixed)
        return jnp.zeros((count,), jnp.int32).at[sequence[jnp.where(places < fixed, places, passed)]].set(jnp.asarray(tallies, jnp.int32))

    tallies = jnp.where(number % 4 == 0, named(heavy_load, number // 4), named(common, number - number // 4 - 1))
    mixed = jax.random.permutation(jax.random.fold_in(own, 3), count)
    source_of, taker = mixed[0:count // 2 * 2:2], mixed[1:count // 2 * 2:2]
    room = jnp.minimum(tallies[source_of] - 1, reach - tallies[taker]) // 2
    room = jnp.where((source_of == sequence[0]) | (taker == sequence[0]) | (tallies[taker] == 0), 0, jnp.maximum(room, 0))
    passed = jax.random.randint(jax.random.fold_in(own, 4), (count // 2,), 0, 1 << 20) % (room + 1)
    tallies = tallies.at[source_of].add(-passed).at[taker].add(passed)
    labels = jnp.searchsorted(jnp.cumsum(tallies), jnp.arange(rows * top), side="right").astype(jnp.int32)
    table = labels.reshape(top, rows).T
    table = table[jax.random.permutation(jax.random.fold_in(own, 1), rows)]
    offset_by = jax.random.randint(jax.random.fold_in(own, 2), (rows, 1), 0, top)
    return jnp.take_along_axis(table, (jnp.arange(top)[None, :] + offset_by) % top, axis=1)


def portions_of(count, total, most, skew, full):
    loads = [(1 << 20) // math.isqrt(rank ** skew) + 1 for rank in range(1, count + 1)]
    largest = most if full else min(most, max(-(-total // count), total * loads[0] // sum(loads)))
    least = 1 if total - largest >= count - 1 else 0
    given, rest = [largest] + [least] * (count - 1), total - largest - least * (count - 1)
    while rest > 0:
        candidates = [i for i in range(1, count) if given[i] < largest] or [i for i in range(1, count) if given[i] < most]
        whole, budget = sum([loads[i] for i in candidates]), rest
        for i in candidates:
            addition = min(most - given[i], max(1, budget * loads[i] // whole), rest)
            given[i] = given[i] + addition
            rest = rest - addition
    return np.array(given)


def gaussian(key, dims, width, bound, cuts=(), held_as=jnp.bfloat16):
    result = width * jax.random.normal(key, dims, jnp.float32)
    if cuts:
        result = result * steps_of(key, dims, cuts, -0.22, 0.18)
    return jnp.clip(result, -bound, bound).astype(held_as)


def setup_inputs(seed: int = 0) -> dict:
    arg_keys = jax.random.split(jax.random.key(seed), 7)
    tokens = gaussian(arg_keys[0], (TOKENS, D), 1.0, 6.0, ((0, 8),))
    expert_ids_keys = jax.random.split(jax.random.fold_in(arg_keys[1], 1), TOKENS // TOK_DEV)
    expert_ids_turns = jax.random.permutation(jax.random.fold_in(arg_keys[1], 3), TOKENS // TOK_DEV)
    expert_ids = jax.vmap(lambda own, number: routed_block(jax.random.fold_in(arg_keys[1], 2), own, number, TOK_DEV, EXPERTS, TOP, CAP, 2))(expert_ids_keys, expert_ids_turns).reshape((TOKENS, TOP))
    gate_weights = jnp.clip(0.19921875 + 0.80078125 * jax.random.uniform(arg_keys[2], (TOKENS, TOP), jnp.float32) ** steps_of(arg_keys[2], (TOKENS, TOP), ((0, 8),), -0.2, 0.2), 0.19921875, 1.0).astype(jnp.bfloat16)
    w_gate = gaussian(arg_keys[3], (EXPERTS, D, FF), D ** -0.5, 0.0625, ((0, 8), (2, 4)))
    w_up = gaussian(arg_keys[4], (EXPERTS, D, FF), D ** -0.5, 0.0625, ((0, 8), (2, 4)))
    w_down = gaussian(arg_keys[5], (EXPERTS, FF, D), FF ** -0.5, 0.125, ((0, 8), (1, 4)))
    return {"tokens": tokens, "expert_ids": expert_ids, "gate_weights": gate_weights, "w_gate": w_gate, "w_up": w_up, "w_down": w_down}


def reference(tokens, expert_ids, gate_weights, w_gate, w_up, w_down):
    pair_count = TOKENS * TOP
    flat_expert = expert_ids.reshape(-1).astype(jnp.int32)
    flat_token = (jnp.arange(pair_count, dtype=jnp.int32) // TOP).astype(jnp.int32)
    flat_gate = gate_weights.reshape(-1).astype(jnp.float32)
    sorted_order = jnp.argsort(flat_expert, stable=True).astype(jnp.int32)
    expert_hits = jnp.sum((flat_expert[:, None] == jnp.arange(EXPERTS, dtype=jnp.int32)[None, :]).astype(jnp.int32), axis=0)
    start_rows = (jnp.cumsum(expert_hits) - expert_hits).astype(jnp.int32)
    padded_rows = (TOKENS // TOK_DEV) * CAP
    sorted_token = jnp.concatenate([flat_token[sorted_order], jnp.full((padded_rows,), TOKENS, jnp.int32)])
    sorted_gate = jnp.concatenate([flat_gate[sorted_order], jnp.zeros((padded_rows,), jnp.float32)])
    padded_tokens = jnp.concatenate([tokens, jnp.zeros((1, D), tokens.dtype)], axis=0)
    shard_width = FF // N_DP

    def scan_step(running, scan_item):
        expert, gate_matrix, up_matrix, down_matrix = scan_item
        token_index = lax.dynamic_slice(sorted_token, (start_rows[expert].astype(jnp.int32),), (padded_rows,))
        weight = lax.dynamic_slice(sorted_gate, (start_rows[expert].astype(jnp.int32),), (padded_rows,))
        live_rows = jnp.arange(padded_rows, dtype=jnp.int32) < expert_hits[expert]
        token_index = jnp.where(live_rows, token_index, TOKENS).astype(jnp.int32)
        weight = jnp.where(live_rows, weight, jnp.zeros_like(weight))
        gathered = jnp.take(padded_tokens, token_index, axis=0)
        gate_proj = jnp.dot(gathered, gate_matrix, preferred_element_type=jnp.float32)
        up_proj = jnp.dot(gathered, up_matrix, preferred_element_type=jnp.float32)
        hidden = (jax.nn.silu(gate_proj) * up_proj).astype(jnp.bfloat16)
        summed = jnp.zeros((padded_rows, D), jnp.float32)
        for part_number in range(N_DP):
            lower = part_number * shard_width
            upper = lower + shard_width
            partial_value = jnp.dot(hidden[:, lower:upper], down_matrix[lower:upper], preferred_element_type=jnp.float32)
            rounded = lax.optimization_barrier(partial_value.astype(jnp.bfloat16))
            summed = summed + rounded.astype(jnp.float32)
        running = running.at[token_index].add(weight[:, None] * summed)
        return running, None

    start = jnp.zeros((TOKENS + 1, D), jnp.float32)
    running, unused = lax.scan(scan_step, start, (jnp.arange(EXPERTS, dtype=jnp.int32), w_gate, w_up, w_down))
    return running[:TOKENS].astype(jnp.bfloat16)
```

```python
import functools

import jax
import jax.numpy as jnp
from jax import lax
from jax.experimental import pallas as pl
from jax.experimental.pallas import tpu as pltpu
from jax.sharding import PartitionSpec as P

CAP = 24
META = 128

BF16 = jnp.bfloat16
F32 = jnp.float32


def dot(a, b):
    return jnp.dot(a, b, preferred_element_type=F32)


def up_kernel(
    experts,
    slots,
    top,
    place,
    meta_ref,
    own0,
    own1,
    far0,
    far1,
    gate_w,
    up_w,
    hidden_ref,
    mix_ref,
    pick,
    gate_acc,
    up_acc,
):
    column, number = pl.program_id(0), pl.program_id(1)
    rows = own0.shape[-2]

    @pl.when((column == 0) & (number == 0))
    def _():
        first = place[2] * experts
        lane = lax.broadcasted_iota(jnp.int32, (rows, META), 1)
        before = (
            lax.broadcasted_iota(jnp.int32, (rows, rows), 1)
            < lax.broadcasted_iota(jnp.int32, (rows, rows), 0)
        ).astype(BF16)
        wide = lax.broadcasted_iota(jnp.int32, (rows, experts * slots), 1)
        for half in range(2):
            ids = meta_ref[half, :, :top].astype(F32)
            weights = meta_ref[half, :, top : 2 * top].astype(F32)
            hits = jnp.zeros((rows, META), F32)
            value = []
            for e in range(experts):
                same = ids == (first + e).astype(F32)
                hit = jnp.sum(same.astype(F32), axis=1, keepdims=True)
                value.append(jnp.sum(jnp.where(same, weights, 0.0), axis=1, keepdims=True))
                hits = jnp.where(lane == e, hit, hits)
            rank = dot(before, hits.astype(BF16))
            target = jnp.full((rows, experts * slots), -1.0, F32)
            scale = jnp.zeros((rows, experts * slots), F32)
            for e in range(experts):
                mine = (wide >= e * slots) & (wide < (e + 1) * slots)
                at = jnp.where(hits[:, e : e + 1] > 0.0, rank[:, e : e + 1] + float(e * slots), -1.0)
                target = jnp.where(mine, at, target)
                scale = jnp.where(mine, value[e], scale)
            chosen = target == wide.astype(F32)
            mix_ref[half] = jnp.where(chosen, scale, 0.0).astype(BF16)
            pick[half] = jnp.transpose(chosen.astype(F32)).astype(BF16)

    def step(x0, x1):
        at = pl.ds(pl.multiple_of(number * slots, 8), slots)
        gathered = jnp.concatenate(
            [
                dot(pick[0, at, :], x0[...].reshape(x0.shape[-2:])).astype(BF16),
                dot(pick[1, at, :], x1[...].reshape(x1.shape[-2:])).astype(BF16),
            ],
            axis=0,
        )
        gate = dot(gathered, gate_w[...])
        up = dot(gathered, up_w[...])

        @pl.when(column == 0)
        def _():
            gate_acc[number] = gate
            up_acc[number] = up

        @pl.when(column > 0)
        def _():
            gate_acc[number] += gate
            up_acc[number] += up

    @pl.when(column < 2)
    def _():
        step(own0, own1)

    @pl.when(column >= 2)
    def _():
        step(far0, far1)

    @pl.when(column == pl.num_programs(0) - 1)
    def _():
        gate = gate_acc[number]
        hidden_ref[...] = (gate / (1.0 + jnp.exp(-gate)) * up_acc[number]).astype(BF16)


def quarter(column, place):
    far, side = column // 2, column % 2
    c = jnp.where(far == 1, 1 - place[0], place[0])
    x = jnp.where(side == 1, 1 - place[1], place[1])
    return x * 2 + c


def spot(role, side, half):
    return jnp.where(role == 0, side, half), jnp.where(role == 0, half, side)


def up_call(place, meta, own, far, gate_w, up_w, slots, top):
    experts, width, hidden = gate_w.shape
    rows, part = own.shape[-2:]

    def own_at(half):
        def at(column, number, place):
            a, b = spot(place[0], jnp.minimum(column, 1), half)
            return a, b, 0, 0

        return pl.BlockSpec((None, None, rows, part), at)

    def far_at(half):
        def at(column, number, place):
            a, b = spot(1 - place[0], jnp.maximum(column - 2, 0), half)
            return a, b, 0, 0

        return pl.BlockSpec((None, None, rows, part), at)

    weight = pl.BlockSpec(
        (None, part, hidden), lambda column, number, place: (number, quarter(column, place), 0)
    )
    return pl.pallas_call(
        functools.partial(up_kernel, experts, slots, top),
        grid_spec=pltpu.PrefetchScalarGridSpec(
            num_scalar_prefetch=1,
            grid=(width // part, experts),
            in_specs=[
                pl.BlockSpec((2, rows, META), lambda column, number, place: (0, 0, 0)),
                own_at(0),
                own_at(1),
                far_at(0),
                far_at(1),
                weight,
                weight,
            ],
            out_specs=[
                pl.BlockSpec(
                    (None, 2 * slots, hidden),
                    lambda column, number, place: (
                        jnp.where(column == width // part - 1, number, 0),
                        0,
                        0,
                    ),
                ),
                pl.BlockSpec(
                    (2, rows, experts * slots), lambda column, number, place: (0, 0, 0)
                ),
            ],
            scratch_shapes=[
                pltpu.VMEM((2, experts * slots, rows), BF16),
                pltpu.VMEM((experts, 2 * slots, hidden), F32),
                pltpu.VMEM((experts, 2 * slots, hidden), F32),
            ],
        ),
        out_shape=[
            jax.ShapeDtypeStruct((experts, 2 * slots, hidden), BF16),
            jax.ShapeDtypeStruct((2, rows, experts * slots), BF16),
        ],
        cost_estimate=pl.CostEstimate(
            flops=8 * experts * slots * width * hidden,
            bytes_accessed=4 * experts * width * hidden,
            transcendentals=0,
        ),
        name="up",
    )(place, meta, own, own, far, far, gate_w, up_w)


def down_kernel(
    experts, slots, place, hidden_ref, mix_ref, down_w, keep_ref, give_ref, result, ready, sems
):
    column, number = pl.program_id(0), pl.program_id(1)
    columns = pl.num_programs(0)
    slot = lax.rem(column, 2)
    value = dot(hidden_ref[number], down_w[...]).astype(BF16)
    at = pl.ds(pl.multiple_of(number * slots, 8), slots)
    result[0, at, :] = value[:slots]
    result[1, at, :] = value[slots:]

    def copy(column, half):
        slot = lax.rem(column, 2)
        side = lax.rem(column, 2)

        def give():
            a, b = spot(1 - place[0], side, half)
            return pltpu.make_async_copy(
                ready.at[slot, half], give_ref.at[a, b], sems.at[slot, half]
            )

        def keep():
            a, b = spot(place[0], side, half)
            return pltpu.make_async_copy(
                ready.at[slot, half], keep_ref.at[a, b], sems.at[slot, half]
            )

        return give, keep

    @pl.when(number == experts - 1)
    def _():
        for half in range(2):

            @pl.when(column >= 2)
            def _():
                copy(column - 2, half)[0]().wait()

            ready[slot, half] = dot(mix_ref[half], result[half]).astype(BF16)
            give, keep = copy(column, half)

            @pl.when(column < 2)
            def _():
                give().start()

            @pl.when(column >= 2)
            def _():
                keep().start()

        @pl.when(column == columns - 1)
        def _():
            for half in range(2):
                copy(column - 1, half)[1]().wait()
                copy(column, half)[1]().wait()


def down_call(place, hidden, mix, down_w, slots):
    experts, depth, width = down_w.shape
    rows = mix.shape[1]
    part = width // 4
    shape = jax.ShapeDtypeStruct((2, 2, rows, part), BF16)
    return pl.pallas_call(
        functools.partial(down_kernel, experts, slots),
        grid_spec=pltpu.PrefetchScalarGridSpec(
            num_scalar_prefetch=1,
            grid=(4, experts),
            in_specs=[
                pl.BlockSpec((experts, 2 * slots, depth), lambda column, number, place: (0, 0, 0)),
                pl.BlockSpec(
                    (2, rows, experts * slots), lambda column, number, place: (0, 0, 0)
                ),
                pl.BlockSpec(
                    (None, depth, part),
                    lambda column, number, place: (
                        number,
                        0,
                        quarter(jnp.where(column < 2, column + 2, column - 2), place),
                    ),
                ),
            ],
            out_specs=[pl.BlockSpec(memory_space=pl.ANY), pl.BlockSpec(memory_space=pl.ANY)],
            scratch_shapes=[
                pltpu.VMEM((2, experts * slots, part), BF16),
                pltpu.VMEM((2, 2, rows, part), BF16),
                pltpu.SemaphoreType.DMA((2, 2)),
            ],
        ),
        out_shape=[shape, shape],
        cost_estimate=pl.CostEstimate(
            flops=4 * experts * slots * width * depth,
            bytes_accessed=2 * experts * width * depth,
            transcendentals=0,
        ),
        name="down",
    )(place, hidden, mix, down_w)


def body(tokens, expert_ids, gate_weights, w_gate, w_up, w_down):
    count, width = tokens.shape
    groups, lanes = lax.axis_size("expert"), lax.axis_size("dp")
    top = expert_ids.shape[1]
    part = width // lanes
    ring = groups // 2
    slots = ring * CAP
    turn = list(range(0, ring, 2))[:1] + list(range(1, ring, 2)) + list(range(0, ring, 2))[:0:-1]

    def every(move):
        pairs = []
        for z in range(ring):
            for y in range(2):
                for x in range(2):
                    for c in range(2):
                        a, b, d, e = move(z, y, x, c)
                        pairs.append((((z * 2 + y) * 2 + x) * 2 + c, ((a * 2 + b) * 2 + d) * 2 + e))
        return pairs

    def send(value, move):
        return lax.ppermute(value, ("expert", "dp"), every(move))

    def along(step):
        def move(z, y, x, c):
            return turn[(turn.index(z) + step) % ring], y, x, c

        return move

    def first(z, y, x, c):
        return (z, y, 1 - x, c) if c == 0 else (z, 1 - y, x, c)

    def second(z, y, x, c):
        return (z, 1 - y, x, c) if c == 0 else (z, y, 1 - x, c)

    def other_x(z, y, x, c):
        return z, y, 1 - x, c

    def other_core(z, y, x, c):
        return z, y, x, 1 - c

    lane = lax.axis_index("dp")
    core, side, group = lane % 2, lane // 2, lax.axis_index("expert")
    place = jnp.stack([core, side, group]).astype(jnp.int32)

    meta = jnp.concatenate(
        [
            expert_ids.astype(BF16),
            gate_weights,
            jnp.zeros((count, META - 2 * top), BF16),
        ],
        axis=1,
    )
    piece = jnp.concatenate([lax.dynamic_slice_in_dim(tokens, lane * part, part, 1), meta], axis=1)
    arrived = [piece] + [send(piece, along(step)) for step in range(1, ring)]
    line = jnp.concatenate(arrived, axis=0)
    crossed = send(line, second)
    pair = jnp.stack([line, crossed])
    wide = jnp.concatenate([pair[None], send(pair, first)[None]], axis=0)
    far = send(wide, other_core)
    tags = jnp.stack(
        [
            line[:, part:],
            jnp.where(core == 0, wide[0, 1, :, part:], wide[1, 0, :, part:]),
        ]
    )
    own, far = wide[..., :part], far[..., :part]

    hidden, mix = up_call(place, tags, own, far, w_gate, w_up, slots, top)
    keep, give = down_call(place, hidden, mix, w_down, slots)

    total = keep.astype(F32) + send(give, other_core).astype(F32)
    total = total.astype(BF16)
    total = (total[0].astype(F32) + send(total[1], first).astype(F32)).astype(BF16)
    total = (total[0].astype(F32) + send(total[1], second).astype(F32)).astype(BF16)
    total = total.reshape(ring, count, part)
    result = total[0].astype(F32)
    for step in range(1, ring):
        result = result + send(total[step], along(ring - step)).astype(F32)
    result = result.astype(BF16)

    two = jnp.where(
        side == 0,
        jnp.stack([result, send(result, other_x)]),
        jnp.stack([send(result, other_x), result]),
    )
    back = send(two, other_core)
    four = jnp.where(core == 0, jnp.stack([two, back], axis=1), jnp.stack([back, two], axis=1))
    return jnp.transpose(four.reshape(lanes, count, part), (1, 0, 2)).reshape(count, width)


def solution(mesh):
    placed = (
        P("expert", None),
        P("expert", None),
        P("expert", None),
        P("expert", None, "dp"),
        P("expert", None, "dp"),
        P("expert", "dp", None),
    )
    return jax.shard_map(
        body, mesh=mesh, in_specs=placed, out_specs=P("expert", None), check_vma=False
    )
```
